32 devices in a mesh: grp: 4 (over x, core), dev: 8 (over z, y).
Axes of the slice: x: 2, y: 2, z: 4, core: 2. Of those that a mesh axis runs over, the one named last changes fastest.
Arguments:
- features: bfloat16 [24576, 512], P(('grp', 'dev')), may hold values from -6 to 6
- grad_out: bfloat16 [24576, 512], P(('grp', 'dev')), may hold values from -6 to 6
- w_self: bfloat16 [512, 512], replicated, may hold values from -0.25 to 0.25
- w_neigh: bfloat16 [512, 512], replicated, may hold values from -0.25 to 0.25
- neighbours: int32 [24576, 32], P(('grp', 'dev')), may hold values from 0 to 895, as said below
- degree: int32 [24576], P(('grp', 'dev')), may hold values from 8 to 32
- send_rows: int32 [256, 8], P(('grp', 'dev')), may hold values from 0 to 767
- hub_rows: int32 [64], P(('grp', 'dev')), may hold values from 0 to 767, as said below
Outputs:
- output: bfloat16 [24576, 512], P(('grp', 'dev'))
- grad_features: bfloat16 [24576, 512], P(('grp', 'dev'))
The draws below stay inside these ranges and needn't reach their ends.
Inputs may be any that keep to these rules, and one draw needn't show every extreme that they name: `neighbours`: codes below 768 name rows of the node's device, the next 64 name rows listed for it by its group, the last 64 name hub nodes. Slot 0 of every node holds a listed row and slot 1 a hub; every listed row of a device is named by some node of the reading device and every hub by some node. `hub_rows`: the 2 entries of one device are distinct rows of that device.
All inputs are finite; a program needn't handle non-finite values.
Results may differ from the reference program's by a relative error of at most 0.0051.
Values may be sent and summed in bfloat16 or wider, within the bound.
A program may use at most 64 MiB of HBM per device.

```python
import jax
import jax.numpy as jnp
from jax import lax

F = 512
ROWS = 768
K = 32
HALO_PEER = 8
HUB_DEV = 2
NODES = 24576
HALO = 64
HUBS = 64
N_GRP = 4
N_DEV = 8


def draw_neighbours(key, part):
    node_ids = jnp.arange(NODES, dtype=jnp.int32)
    local_ids = node_ids % ROWS
    device_ids = node_ids // ROWS
    keys = jax.random.split(key, 6)
    shift_halo = jax.random.randint(keys[0], (NODES // ROWS,), 0, HALO)
    first_slot = ROWS + (local_ids + shift_halo[device_ids]) % HALO
    shift_hub = jax.random.randint(keys[1], (), 0, HUBS)
    second_slot = ROWS + HALO + (node_ids + shift_hub) % HUBS
    kinds = jax.random.randint(keys[2], (NODES, K - 2), 0, 10)
    local_pick = jax.random.randint(keys[3], (NODES, K - 2), 0, ROWS)
    halo_pick = ROWS + jax.random.randint(keys[4], (NODES, K - 2), 0, HALO)
    hub_pick = ROWS + HALO + jax.random.randint(keys[5], (NODES, K - 2), 0, HUBS)
    remaining = jnp.where(kinds < 5, local_pick, jnp.where(kinds < 8, halo_pick, hub_pick))
    return jnp.concatenate([first_slot[:, None], second_slot[:, None], remaining], axis=1).astype(jnp.int32)


def permute_rows(one_key):
    return jax.random.permutation(one_key, ROWS)


def draw_hub_rows(key, part):
    devices = NODES // ROWS
    keys = jax.random.split(key, devices + 1)
    orders = jax.vmap(permute_rows)(keys[:devices]).astype(jnp.int32)
    first_dev = jax.random.randint(keys[devices], (), 0, devices)
    second_dev = (first_dev + 1) % devices
    dev_ids = jnp.arange(devices, dtype=jnp.int32)
    shifts = jnp.where(dev_ids == first_dev, ROWS - 1 - orders[:, 0], jnp.where(dev_ids == second_dev, -orders[:, 0], 0))
    rotated = (orders + shifts[:, None]) % ROWS
    return rotated[:, :HUB_DEV].reshape(HUBS).astype(jnp.int32)


def plant(drawn, stream_key, least, top_value):
    shape = drawn.shape
    index_at = [jax.random.randint(jax.random.fold_in(stream_key, axis), (), 0, shape[axis]) for axis in range(len(shape))]
    drawn = drawn.at[tuple(index_at)].set(least)
    longest = shape.index(max(shape))
    index_at[longest] = (index_at[longest] + 1) % shape[longest]
    return drawn.at[tuple(index_at)].set(top_value)


def shard_levels(own_key, dims, cuts, low, top_value):
    def one(position, parts):
        steps = jax.random.uniform(jax.random.fold_in(jax.random.fold_in(own_key, 6), position), (parts,), jnp.float32, low / len(cuts), top_value / len(cuts))
        return jnp.repeat(jnp.exp(steps), dims[position] // parts).reshape((-1,) + (1,) * (len(dims) - position - 1))

    loudness = one(*cuts[0])
    for cut in cuts[1:]:
        loudness = loudness * one(*cut)
    return loudness


def centred(rng, dims, scale, most, cuts=(), kind=jnp.bfloat16):
    values = scale * jax.random.normal(rng, dims, jnp.float32)
    if cuts:
        values = values * shard_levels(rng, dims, cuts, -0.22, 0.18)
    return jnp.clip(values, -most, most).astype(kind)


def setup_inputs(seed: int = 0) -> dict:
    streams_of = jax.random.split(jax.random.key(seed), 9)
    return {
        "features": centred(streams_of[0], (NODES, F), 1.0, 6.0, ((0, 32),)),
        "grad_out": centred(streams_of[1], (NODES, F), 1.0, 6.0, ((0, 32),)),
        "w_self": centred(streams_of[2], (F, F), F ** -0.5, 0.25),
        "w_neigh": centred(streams_of[3], (F, F), F ** -0.5, 0.25),
        "neighbours": draw_neighbours(jax.random.fold_in(streams_of[8], 71), 0),
        "degree": plant(jax.random.randint(streams_of[5], (NODES,), K // 4, K + 1), jax.random.fold_in(streams_of[5], 1), K // 4, K).astype(jnp.int32),
        "send_rows": plant(jax.random.randint(streams_of[6], (N_GRP * N_DEV * N_DEV, HALO_PEER), 0, ROWS), jax.random.fold_in(streams_of[6], 1), 0, ROWS - 1).astype(jnp.int32),
        "hub_rows": draw_hub_rows(jax.random.fold_in(streams_of[8], 71), 0),
    }


def sources_of(neighbours, send_rows, hub_rows):
    node_ids = jnp.arange(NODES, dtype=jnp.int32)
    owner_dev = node_ids // ROWS
    group_ids = owner_dev // N_DEV
    member_ids = owner_dev % N_DEV
    local_ids = owner_dev[:, None] * ROWS + neighbours
    halo_codes = jnp.clip(neighbours - ROWS, 0, HALO - 1)
    peer_dev = group_ids[:, None] * N_DEV + halo_codes // HALO_PEER
    send_pos = (peer_dev * N_DEV + member_ids[:, None]) * HALO_PEER + halo_codes % HALO_PEER
    halo_ids = peer_dev * ROWS + send_rows.reshape(-1)[send_pos]
    hub_codes = jnp.clip(neighbours - ROWS - HALO, 0, HUBS - 1)
    hub_ids = (hub_codes // HUB_DEV) * ROWS + hub_rows[hub_codes]
    picked = jnp.where(neighbours < ROWS + HALO, halo_ids, hub_ids)
    return jnp.where(neighbours < ROWS, local_ids, picked).astype(jnp.int32)


def reference(features, grad_out, w_self, w_neigh, neighbours, degree, send_rows, hub_rows):
    source = sources_of(neighbours, send_rows, hub_rows)
    valid_slots = jnp.arange(K, dtype=jnp.int32)[None, :] < degree[:, None]
    blocks = NODES // ROWS
    src_blocks = source.reshape(blocks, ROWS, K)
    mask_blocks = valid_slots.reshape(blocks, ROWS, K)

    def gather_block(block_args):
        block_src, block_mask = block_args
        picked = features[block_src].astype(jnp.float32)
        return jnp.sum(jnp.where(block_mask[:, :, None], picked, jnp.zeros((), jnp.float32)), axis=1)

    summed = lax.map(gather_block, (src_blocks, mask_blocks)).reshape(NODES, F)
    degree_f = degree.astype(jnp.float32)[:, None]
    neigh_mean = (summed / degree_f).astype(jnp.bfloat16)
    preact = jnp.dot(features, w_self, preferred_element_type=jnp.float32) + jnp.dot(neigh_mean, w_neigh, preferred_element_type=jnp.float32)
    output = jax.nn.silu(preact).astype(jnp.bfloat16)
    sigmoid_pre = jax.nn.sigmoid(preact)
    gated = (grad_out.astype(jnp.float32) * sigmoid_pre * (1.0 + preact * (1.0 - sigmoid_pre))).astype(jnp.bfloat16)
    grad_self = jnp.dot(gated, w_self.T, preferred_element_type=jnp.float32)
    scaled = (jnp.dot(gated, w_neigh.T, preferred_element_type=jnp.float32) / degree_f).astype(jnp.bfloat16)
    scaled_blocks = scaled.reshape(blocks, ROWS, F)

    def scatter_block(accumulated, block_args):
        block_src, block_mask, block_scaled = block_args
        contributions = jnp.where(block_mask[:, :, None], block_scaled.astype(jnp.float32)[:, None, :], jnp.zeros((), jnp.float32))
        updated = accumulated.at[block_src.reshape(-1)].add(contributions.reshape(ROWS * K, F))
        return updated, None

    accumulated, unused = lax.scan(scatter_block, jnp.zeros((NODES, F), jnp.float32), (src_blocks, mask_blocks, scaled_blocks))
    grad_features = (grad_self + accumulated).astype(jnp.bfloat16)
    return output, grad_features
```

```python
import math

import jax
import jax.numpy as jnp
from jax import lax
from jax.sharding import PartitionSpec as P


def count_tiles(slot_codes, keep_mask, tile_width, first_code):
    column_ids = first_code + lax.iota(jnp.int32, tile_width)
    matches = (slot_codes[:, :, None] == column_ids[None, None, :]) & keep_mask[:, :, None]
    return jnp.sum(matches.astype(jnp.bfloat16), axis=1)


def local(features, grad_out, w_self, w_neigh, neighbours, degree, send_rows, hub_rows):
    row_count, feat_width = features.shape
    slot_count = neighbours.shape[1]
    groups = lax.axis_size("grp")
    members = lax.axis_size("dev")
    halo_count = send_rows.shape[0] * send_rows.shape[1]
    owned_hubs = hub_rows.shape[0]
    hub_count = owned_hubs * groups * members
    keep_slots = lax.iota(jnp.int32, slot_count)[None, :] < degree[:, None]
    block_rows = math.gcd(row_count, 256)
    block_total = row_count // block_rows

    def build_tiles(block_args):
        slot_codes, keep_mask = block_args
        return (
            count_tiles(slot_codes, keep_mask, row_count, 0),
            count_tiles(slot_codes, keep_mask, halo_count, row_count),
            count_tiles(slot_codes, keep_mask, hub_count, row_count + halo_count),
        )

    tile_local, tile_halo, tile_hub = lax.map(
        build_tiles,
        (
            neighbours.reshape(block_total, block_rows, slot_count),
            keep_slots.reshape(block_total, block_rows, slot_count),
        ),
    )
    tile_local = tile_local.reshape(row_count, row_count)
    tile_halo = tile_halo.reshape(row_count, halo_count)
    tile_hub = tile_hub.reshape(row_count, hub_count)
    send_list = send_rows.reshape(halo_count)
    outgoing = jnp.take(features, send_list, axis=0)
    incoming = lax.all_to_all(outgoing, "dev", split_axis=0, concat_axis=0, tiled=True)
    summed = jnp.dot(tile_local, features, preferred_element_type=jnp.float32)
    summed = summed + jnp.dot(tile_halo, incoming, preferred_element_type=jnp.float32)
    hub_own = jnp.take(features, hub_rows, axis=0)
    tile_cols = tile_hub
    summed = summed + jnp.dot(
        tile_cols,
        lax.all_to_all(
            jnp.tile(hub_own, (groups * members, 1)), ("grp", "dev"), split_axis=0, concat_axis=0, tiled=True
        ),
        preferred_element_type=jnp.float32,
    )
    degree_f = degree.astype(jnp.float32)[:, None]
    neigh_mean = (summed / degree_f).astype(jnp.bfloat16)
    preact = jnp.dot(features, w_self, preferred_element_type=jnp.float32) + jnp.dot(
        neigh_mean, w_neigh, preferred_element_type=jnp.float32
    )
    output = jax.nn.silu(preact).astype(jnp.bfloat16)
    sigmoid_pre = jax.nn.sigmoid(preact)
    gated = (
        grad_out.astype(jnp.float32) * sigmoid_pre * (1.0 + preact * (1.0 - sigmoid_pre))
    ).astype(jnp.bfloat16)
    contract_last = (((1,), (1,)), ((), ()))
    contract_first = (((0,), (0,)), ((), ()))
    grad_self = lax.dot_general(gated, w_self, contract_last, preferred_element_type=jnp.float32)
    scaled = (
        lax.dot_general(gated, w_neigh, contract_last, preferred_element_type=jnp.float32)
        / degree_f
    ).astype(jnp.bfloat16)
    grad_total = grad_self + lax.dot_general(
        tile_local, scaled, contract_first, preferred_element_type=jnp.float32
    )
    halo_partial = lax.dot_general(
        tile_halo, scaled, contract_first, preferred_element_type=jnp.float32
    )
    returned = lax.all_to_all(
        halo_partial.astype(jnp.bfloat16), "dev", split_axis=0, concat_axis=0, tiled=True
    ).astype(halo_partial.dtype)
    grad_total = grad_total + jax.ops.segment_sum(returned, send_list, num_segments=row_count)
    tile_cols = tile_hub
    hub_partial = lax.dot_general(tile_cols, scaled, contract_first, preferred_element_type=jnp.float32)
    arrived = lax.all_to_all(hub_partial, ("grp", "dev"), split_axis=0, concat_axis=0, tiled=True)
    mine = jnp.sum(arrived.reshape(groups * members, owned_hubs, feat_width), axis=0)
    grad_total = grad_total + jax.ops.segment_sum(mine, hub_rows, num_segments=row_count)
    return (output, grad_total.astype(jnp.bfloat16))


def solution(mesh):
    placed = (
        P(("grp", "dev"), None),
        P(("grp", "dev"), None),
        P(),
        P(),
        P(("grp", "dev"), None),
        P(("grp", "dev")),
        P(("grp", "dev"), None),
        P(("grp", "dev")),
    )
    return jax.shard_map(
        local,
        mesh=mesh,
        in_specs=placed,
        out_specs=(P(("grp", "dev"), None), P(("grp", "dev"), None)),
        check_vma=False,
    )
```

```python
import functools

import jax
import jax.numpy as jnp
from jax import lax
from jax.experimental import pallas as pl
from jax.experimental.pallas import tpu as pltpu
from jax.sharding import PartitionSpec as P

MESH = pl.DeviceIdType.MESH
BF = jnp.bfloat16
F32 = jnp.float32
CODE = jnp.int16
PACK = 16


def dot(a, b, lhs_dim, rhs_dim):
    return lax.dot_general(a, b, (((lhs_dim,), (rhs_dim,)), ((), ())), preferred_element_type=F32)


def layer_kernel(
    groups, members, owned, tile_rows,
    x_ref, g_ref, ws_ref, wn_ref, codes_ref, deg_ref, send_ref, hub_ref,
    out_ref, grad_ref,
    counts, source, scaled, total, spread,
    halo_out, halo_in, back_out, back_in, hub_out, hub_in, sum_out, sum_in,
    send_sems, recv_sems,
):
    rows, feat = x_ref.shape
    slots = codes_ref.shape[0]
    devices = groups * members
    peer_rows = halo_out.shape[1]
    halo = members * peer_rows
    hubs = owned * devices
    first_hub = rows + halo
    columns = first_hub + hubs
    me_g, me_m = lax.axis_index("grp"), lax.axis_index("dev")
    me = me_g * members + me_m

    barrier = pltpu.get_barrier_semaphore()

    def greet(step, carry):
        t = lax.rem(me + step, devices)
        pl.semaphore_signal(barrier, inc=1, device_id=(t // members, lax.rem(t, members)), device_id_type=MESH)
        return carry

    lax.fori_loop(1, devices, greet, 0)

    row_ids = lax.broadcasted_iota(jnp.int32, (halo, rows), 1)
    pick_halo = jnp.where(row_ids == send_ref[...], 1.0, 0.0).astype(BF)
    halo_out[...] = dot(pick_halo, x_ref[...], 1, 0).reshape(members, peer_rows, feat)
    lane_ids = lax.broadcasted_iota(jnp.int32, (8, rows), 1)
    sub_ids = lax.broadcasted_iota(jnp.int32, (8, rows), 0)
    hub_mask = jnp.zeros((8, rows), F32)
    for j in range(owned):
        hub_mask = jnp.where((sub_ids == j) & (lane_ids == hub_ref[j]), 1.0, hub_mask)
    own = dot(hub_mask.astype(BF), x_ref[...], 1, 0)
    for j in range(owned):
        hub_out[0, :, j * feat:(j + 1) * feat] = own[j:j + 1, :]
    hub_in[me] = hub_out[0]
    halo_in[me_m] = halo_out[me_m]
    source[:rows, :] = x_ref[...]
    for k in range(slots):
        spread[k] = jnp.broadcast_to(codes_ref[k:k + 1, :], (PACK, rows)).astype(CODE)

    pl.semaphore_wait(barrier, devices - 1)

    def to_member(src, dst, sem):
        def body(step, carry):
            p = lax.rem(me_m + step, members)
            pltpu.make_async_remote_copy(
                src_ref=src.at[p], dst_ref=dst.at[me_m], send_sem=send_sems.at[sem], recv_sem=recv_sems.at[sem],
                device_id=(me_g, p), device_id_type=MESH,
            ).start()
            return carry
        lax.fori_loop(1, members, body, 0)

    def to_all(src, dst, sem, shared):
        def body(step, carry):
            t = lax.rem(me + step, devices)
            pltpu.make_async_remote_copy(
                src_ref=src.at[0 if shared else t], dst_ref=dst.at[me],
                send_sem=send_sems.at[sem], recv_sem=recv_sems.at[sem],
                device_id=(t // members, lax.rem(t, members)), device_id_type=MESH,
            ).start()
            return carry
        lax.fori_loop(1, devices, body, 0)

    def drain(buf, count, sem):
        view = buf.at[pl.ds(0, count)]
        pltpu.make_async_copy(view, view, recv_sems.at[sem]).wait()
        pltpu.make_async_copy(view, view, send_sems.at[sem]).wait()

    to_all(hub_out, hub_in, 1, True)
    to_member(halo_out, halo_in, 0)

    parts = tile_rows // PACK
    sub = lax.broadcasted_iota(jnp.int32, (PACK, rows), 0)

    def count_block(i, carry):
        base = pl.multiple_of(i * tile_rows, tile_rows)
        names = [(sub + (base + PACK * q)).astype(CODE) for q in range(parts)]
        one, zero = jnp.ones((PACK, rows), BF), jnp.zeros((PACK, rows), BF)
        sums = [zero] * parts
        for k in range(slots):
            code = spread[k]
            sums = [s + jnp.where(code == n, one, zero) for s, n in zip(sums, names)]
        for q in range(parts):
            counts[pl.ds(pl.multiple_of(base + PACK * q, PACK), PACK), :] = sums[q]
        return carry

    lax.fori_loop(0, columns // tile_rows, count_block, 0)

    drain(halo_in, members - 1, 0)
    drain(hub_in, devices - 1, 1)
    source[rows:first_hub, :] = halo_in[...].reshape(halo, feat).astype(BF)
    hub_rows_in = hub_in[...].reshape(devices, owned * feat)
    for j in range(owned):
        source[first_hub + j * devices:first_hub + (j + 1) * devices, :] = (
            hub_rows_in[:, j * feat:(j + 1) * feat].astype(BF))

    block = 256 if rows % 256 == 0 else rows
    blocks = rows // block

    def node_block(i, carry):
        at = pl.ds(pl.multiple_of(i * block, block), block)
        degree = deg_ref[at, :]
        mean = (dot(counts[:, at], source[...], 0, 0) / degree).astype(BF)
        pre = dot(x_ref[at, :], ws_ref[...], 1, 0) + dot(mean, wn_ref[...], 1, 0)
        sig = jax.nn.sigmoid(pre)
        out_ref[at, :] = (pre * sig).astype(BF)
        gated = (g_ref[at, :].astype(F32) * sig * (1.0 + pre * (1.0 - sig))).astype(BF)
        scaled[at, :] = (dot(gated, wn_ref[...], 1, 1) / degree).astype(BF)
        total[at, :] = dot(gated, ws_ref[...], 1, 1)
        return carry

    lax.fori_loop(0, blocks, node_block, 0)

    away = dot(counts[rows:, :], scaled[...], 1, 0)
    back_out[...] = away[:halo].reshape(members, peer_rows, feat)
    sum_out[...] = jnp.concatenate(
        [away[halo + j * devices:halo + (j + 1) * devices] for j in range(owned)], axis=1
    ).reshape(devices, 1, owned * feat)
    back_in[me_m] = back_out[me_m]
    sum_in[me] = sum_out[me]

    def local_block(i, carry):
        at = pl.ds(pl.multiple_of(i * block, block), block)
        total[at, :] += dot(counts[at, :], scaled[...], 1, 0)
        return carry

    lax.fori_loop(0, 1, local_block, 0)
    to_all(sum_out, sum_in, 3, False)
    to_member(back_out, back_in, 2)
    lax.fori_loop(1, blocks, local_block, 0)
    drain(back_in, members - 1, 2)
    drain(sum_in, devices - 1, 3)

    returned = back_in[...].reshape(halo, feat).astype(BF)
    mine = jnp.sum(sum_in[...], axis=0)

    def final_block(i, carry):
        at = pl.ds(pl.multiple_of(i * block, block), block)
        ids = lax.broadcasted_iota(jnp.int32, (halo, block), 1) + i * block
        place = jnp.where(ids == send_ref[...], 1.0, 0.0).astype(BF)
        value = total[at, :] + dot(place, returned, 0, 0)
        node_ids = lax.broadcasted_iota(jnp.int32, (block, feat), 0) + i * block
        for j in range(owned):
            value = value + jnp.where(node_ids == hub_ref[j], mine[:, j * feat:(j + 1) * feat], 0.0)
        grad_ref[at, :] = value.astype(BF)
        return carry

    lax.fori_loop(0, blocks, final_block, 0)


def local(groups, members, features, grad_out, w_self, w_neigh, neighbours, degree, send_rows, hub_rows):
    rows, feat = features.shape
    slots = neighbours.shape[1]
    devices = groups * members
    peer_rows = send_rows.shape[1]
    halo = send_rows.shape[0] * peer_rows
    owned = hub_rows.shape[0]
    hubs = owned * devices
    first_hub = rows + halo
    columns = first_hub + hubs
    h = neighbours - first_hub
    codes = jnp.where(h >= 0, first_hub + (h % owned) * devices + h // owned, neighbours)
    codes = jnp.where(lax.iota(jnp.int32, slots)[None, :] < degree[:, None], codes, -1).T
    vmem = pl.BlockSpec(memory_space=pltpu.VMEM)
    chunk = (members, peer_rows, feat)
    strip = (devices, 1, owned * feat)
    return pl.pallas_call(
        functools.partial(layer_kernel, groups, members, owned, 64),
        out_shape=(jax.ShapeDtypeStruct((rows, feat), BF), jax.ShapeDtypeStruct((rows, feat), BF)),
        in_specs=[vmem] * 7 + [pl.BlockSpec(memory_space=pltpu.SMEM)],
        out_specs=(vmem, vmem),
        scratch_shapes=[
            pltpu.VMEM((columns, rows), BF),
            pltpu.VMEM((columns, feat), BF),
            pltpu.VMEM((rows, feat), BF),
            pltpu.VMEM((rows, feat), F32),
            pltpu.VMEM((slots, PACK, rows), CODE),
            pltpu.VMEM(chunk, F32), pltpu.VMEM(chunk, F32), pltpu.VMEM(chunk, F32), pltpu.VMEM(chunk, F32),
            pltpu.VMEM((1, 1, owned * feat), F32), pltpu.VMEM(strip, F32), pltpu.VMEM(strip, F32), pltpu.VMEM(strip, F32),
            pltpu.SemaphoreType.DMA((4,)),
            pltpu.SemaphoreType.DMA((4,)),
        ],
        compiler_params=pltpu.CompilerParams(collective_id=0, has_side_effects=True),
    )(
        features, grad_out, w_self, w_neigh, codes,
        degree.astype(F32)[:, None], send_rows.reshape(halo, 1), hub_rows,
    )


def solution(mesh):
    both = ("grp", "dev")
    placed = (P(both, None), P(both, None), P(), P(), P(both, None), P(both), P(both, None), P(both))
    return jax.shard_map(
        functools.partial(local, mesh.shape["grp"], mesh.shape["dev"]),
        mesh=mesh,
        in_specs=placed,
        out_specs=(P(both, None), P(both, None)),
        check_vma=False,
    )
```
